32 devices in a mesh: alpha: 8 (over y, x, core), beta: 4 (over z).
Axes of the slice: x: 2, y: 2, z: 4, core: 2. Of those that a mesh axis runs over, the one named last changes fastest.
Arguments:
- vector: float32 [128, 768], P('alpha', 'beta'), may hold values from -6 to 6
- integrals: float32 [196, 196], replicated, may hold values from -0.078125 to 0.078125
- alpha_targets: int32 [56, 128], replicated, may hold values from 0 to 127
- alpha_pairs: int32 [56, 128], replicated, may hold values from 0 to 195
- alpha_signs: int32 [56, 128], replicated, may hold values from -1 to 1, as said below
- beta_targets: int32 [56, 768], replicated, may hold values from 0 to 767
- beta_pairs: int32 [56, 768], replicated, may hold values from 0 to 195
- beta_signs: int32 [56, 768], replicated, may hold values from -1 to 1, as said below
Outputs:
- sigma: float32 [128, 768], P('alpha', 'beta')
The draws below stay inside these ranges and needn't reach their ends.
Inputs may be any that keep to these rules, and one draw needn't show every extreme that they name: `alpha_signs`: every entry is -1 or 1. `beta_signs`: every entry is -1 or 1.
All inputs are finite; a program needn't handle non-finite values.
Results may differ from the reference program's by a relative error of at most 0.0001.
Values sent between devices are 32-bit elements; how exact they have to be, the bound alone decides.
No kernel may reach another device: no remote copies, remote signals or barrier semaphores. Data moves between devices by JAX's collectives and lax.ppermute only.
A program may use at most 64 MiB of HBM per device.

```python
import math
import jax
import jax.numpy as jnp
from jax import lax

EXC = 56
PAIRS = 196
NA = 128
NB = 768


def draw_alpha_signs(key, part):
    return 2 * jax.random.randint(jax.random.fold_in(key, 11), (EXC, NA), 0, 2, dtype=jnp.int32) - 1


def draw_beta_signs(key, part):
    return 2 * jax.random.randint(jax.random.fold_in(key, 23), (EXC, NB), 0, 2, dtype=jnp.int32) - 1


def with_ends(entries, key, low, top_value):
    longest = entries.shape.index(max(entries.shape))
    spots = []
    for shift in (0, 1):
        where = [jax.random.randint(jax.random.fold_in(key, axis), (), 0, length) for axis, length in enumerate(entries.shape)]
        where[longest] = (where[longest] + shift) % entries.shape[longest]
        spots.append(tuple(where))
    return entries.at[spots[0]].set(low).at[spots[1]].set(top_value)


def shard_levels(key, dims, cuts, smallest, top_value):
    factor_of = 1.0
    for dim, parts in cuts:
        draws = jax.random.uniform(jax.random.fold_in(jax.random.fold_in(key, 6), dim), (parts,), jnp.float32, smallest / len(cuts), top_value / len(cuts))
        factor_of = factor_of * jnp.repeat(jnp.exp(draws), dims[dim] // parts).reshape((-1,) + (1,) * (len(dims) - 1 - dim))
    return factor_of


def centred(own_key, extent, width, limit, shards=(), kind=jnp.bfloat16):
    drawn = jax.random.normal(own_key, extent, jnp.float32) * width
    if len(shards) > 0:
        drawn = shard_levels(own_key, extent, shards, -0.22, 0.18) * drawn
    return jnp.clip(drawn, min=-limit, max=limit).astype(kind)


def setup_inputs(seed: int = 0) -> dict:
    streams_of = jax.random.split(jax.random.key(seed), 9)
    vector = centred(streams_of[0], (NA, NB), 1.0, 6.0, ((0, 8), (1, 4)), jnp.float32)
    integrals = centred(streams_of[1], (PAIRS, PAIRS), (2 * EXC * EXC) ** -0.5, 0.078125, (), jnp.float32)
    alpha_targets = with_ends(jax.random.randint(streams_of[2], (EXC, NA), 0, NA), jax.random.fold_in(streams_of[2], 1), 0, NA - 1).astype(jnp.int32)
    alpha_pairs = with_ends(jax.random.randint(streams_of[3], (EXC, NA), 0, PAIRS), jax.random.fold_in(streams_of[3], 1), 0, PAIRS - 1).astype(jnp.int32)
    alpha_signs = draw_alpha_signs(jax.random.fold_in(streams_of[8], 71), 0)
    beta_targets = with_ends(jax.random.randint(streams_of[5], (EXC, NB), 0, NB), jax.random.fold_in(streams_of[5], 1), 0, NB - 1).astype(jnp.int32)
    beta_pairs = with_ends(jax.random.randint(streams_of[6], (EXC, NB), 0, PAIRS), jax.random.fold_in(streams_of[6], 1), 0, PAIRS - 1).astype(jnp.int32)
    beta_signs = draw_beta_signs(jax.random.fold_in(streams_of[8], 71), 0)
    return dict(vector=vector, integrals=integrals, alpha_targets=alpha_targets, alpha_pairs=alpha_pairs, alpha_signs=alpha_signs, beta_targets=beta_targets, beta_pairs=beta_pairs, beta_signs=beta_signs)


def spin_sum(lookup, targets, pairs, signs, integrals):
    col_count = lookup.shape[0]
    strings = targets.shape[0]
    excite = targets.shape[1]
    pair_count = integrals.shape[0]
    block_size = math.gcd(strings, 64)
    block_count = strings // block_size
    string_index = jnp.broadcast_to(jnp.arange(block_size, dtype=jnp.int32)[:, None], (block_size, excite))

    def one_block(collected, block_lists):
        block_targets, block_pairs, block_signs = block_lists
        flat_targets = block_targets.reshape(-1)
        fetched = jnp.take(lookup, flat_targets, axis=1).reshape(col_count, block_size, excite)
        phases = block_signs.astype(lookup.dtype)
        density = jnp.zeros((col_count, block_size, pair_count), lookup.dtype)
        density = density.at[:, string_index, block_pairs].add(fetched * phases[None])
        contracted = jnp.einsum("wsp,qp->wsq", density, integrals, precision=lax.Precision.HIGHEST)
        picked = contracted[:, string_index, block_pairs] * phases[None]
        collected = collected.at[:, flat_targets].add(picked.reshape(col_count, block_size * excite))
        return collected, None

    block_lists = (targets.reshape(block_count, block_size, excite),
                   pairs.reshape(block_count, block_size, excite),
                   signs.reshape(block_count, block_size, excite))
    start_value = jnp.zeros((col_count, lookup.shape[1]), lookup.dtype)
    collected, _ = lax.scan(one_block, start_value, block_lists)
    return collected


def reference(vector, integrals, alpha_targets, alpha_pairs, alpha_signs, beta_targets, beta_pairs, beta_signs):
    alpha_part = spin_sum(vector.T, alpha_targets.T, alpha_pairs.T, alpha_signs.T, integrals).T
    beta_part = spin_sum(vector, beta_targets.T, beta_pairs.T, beta_signs.T, integrals)
    return alpha_part + beta_part
```

```python
import functools

import jax
import jax.numpy as jnp
from jax import lax
from jax.experimental import pallas as pl
from jax.experimental.pallas import tpu as pltpu
from jax.sharding import PartitionSpec as P

LANES = 128
HALF = 64
WIDE = 256
GROUP = 8
F32 = jnp.float32
BF16 = jnp.bfloat16


def nt(left, right):
    return lax.dot_general(left, right, (((1,), (1,)), ((), ())), preferred_element_type=F32)


def nn(left, right):
    return lax.dot_general(left, right, (((1,), (0,)), ((), ())), preferred_element_type=F32)


def parts(value):
    high = value.astype(BF16)
    low = (value - high.astype(F32)).astype(BF16)
    return high, low


def up(size, step):
    return -(-size // step) * step


def local_place(targets, own, block, blocks):
    owner = jnp.zeros_like(targets)
    for step in range(1, blocks):
        owner += (targets >= step * block).astype(jnp.int32)
    return ((owner ^ own) - owner) * block + targets


def pair_table(targets, pairs, signs, own, block, blocks):
    place = local_place(targets, own, block, blocks)
    code = place * 512 + pairs * 2 + (signs < 0).astype(jnp.int32)
    excite, width = code.shape
    filler = jnp.full((HALF - excite, width), 510, jnp.int32)
    return jnp.concatenate([code, filler], axis=0)


def fold(code, strings):
    half = strings // 2
    first = code[:, :LANES]
    second = pltpu.roll(code, (code.shape[1] - half) % code.shape[1], 1)[:, :LANES]
    return jnp.concatenate([first, second], axis=0).T


def fill_integrals(integrals_ref, wide_ref):
    count = integrals_ref.shape[0]
    padded = jnp.pad(integrals_ref[...], ((0, WIDE - count), (0, WIDE - count)))
    high, low = parts(padded)
    if wide_ref.shape[0] == WIDE:
        wide_ref[:, :WIDE] = high
        wide_ref[:, WIDE:] = low
    else:
        wide_ref[:WIDE, :] = high
        wide_ref[WIDE:, :] = low


def contribution(codes, excite, fetch, exact, wide_ref, chunks, chunk_width):
    lane = lax.broadcasted_iota(jnp.int32, (1, LANES), 1)
    real = (lane & (HALF - 1)) < excite
    first = (lane < HALF).astype(F32).astype(BF16)
    second = (lane >= HALF).astype(F32).astype(BF16)
    down = lax.broadcasted_iota(jnp.int32, (WIDE, LANES), 0)
    down_chunk = lax.broadcasted_iota(jnp.int32, (chunk_width, LANES), 0)
    densities = []
    for g in range(GROUP):
        code = codes[g : g + 1, :]
        pair = (code >> 1) & 255
        sign = jnp.where(real, 1 - 2 * (code & 1), 0).astype(F32)
        one_hot = (down == pair).astype(F32).astype(BF16)
        value = fetch(code >> 9) * sign
        rows = value.shape[0]
        if exact:
            held = value.astype(BF16)
            dens = nt(jnp.concatenate([held * first, held * second], axis=0), one_hot)
        else:
            high, low = parts(value)
            stack = jnp.concatenate([high * first, high * second, low * first, low * second], axis=0)
            dens = nt(stack, one_hot)
            dens = dens[: 2 * rows] + dens[2 * rows :]
        densities.append(dens)
    density = jnp.concatenate(densities, axis=0)
    if exact:
        both = nn(density.astype(BF16), wide_ref[...])
        image = both[:, :WIDE] + both[:, WIDE:]
    else:
        high, low = parts(density)
        both = nt(high, wide_ref[...])
        image = both[:, :WIDE] + both[:, WIDE:] + nt(low, wide_ref[:WIDE, :])
    lefts, rights = [], []
    for g in range(GROUP):
        code = codes[g : g + 1, :]
        pair = (code >> 1) & 255
        sign = jnp.where(real, 1 - 2 * (code & 1), 0).astype(F32)
        base = 2 * rows * g
        index = jnp.broadcast_to(pair & (LANES - 1), (rows, LANES))
        upper = pair >= LANES
        picks = []
        for s in range(2):
            block = image[base + s * rows : base + (s + 1) * rows]
            low_pick = jnp.take_along_axis(block[:, :LANES], index, axis=1, mode="promise_in_bounds")
            high_pick = jnp.take_along_axis(block[:, LANES:], index, axis=1, mode="promise_in_bounds")
            picks.append(jnp.where(upper, high_pick, low_pick))
        value = jnp.where(lane < HALF, picks[0], picks[1]) * sign
        high, low = parts(value)
        place = code >> 9
        if chunks == 1:
            lefts.append(jnp.concatenate([high, low], axis=0))
            within = place
        else:
            within = place % chunk_width
            chunk = place // chunk_width
            pieces = []
            for c in range(chunks):
                mask = (chunk == c).astype(F32).astype(BF16)
                pieces += [high * mask, low * mask]
            lefts.append(jnp.concatenate(pieces, axis=0))
        rights.append((down_chunk == within).astype(F32).astype(BF16))
    summed = nt(jnp.concatenate(lefts, axis=1), jnp.concatenate(rights, axis=1))
    return summed


def prepare(excite, rows, block, a_blocks, b_blocks, integrals, at, ap, asn, bt, bp, bsn, codes, matrix, wide, acodes):
    own_a = lax.axis_index("alpha")
    own_b = lax.axis_index("beta")
    fill_integrals(integrals, wide)
    window = min(up(block + LANES - 1, LANES), bt.shape[1])
    start = jnp.minimum(own_b * block // LANES * LANES, bt.shape[1] - window)
    start = pl.multiple_of(start, LANES)
    table = pair_table(bt[:, pl.ds(start, window)], bp[:, pl.ds(start, window)], bsn[:, pl.ds(start, window)], own_b, block, b_blocks)
    table = pltpu.roll(table, (window - (own_b * block - start)) % window, 1)
    codes[...] = fold(table, block)[: codes.shape[0]]
    count = at.shape[1]
    for t in range(count // LANES):
        cut = slice(t * LANES, (t + 1) * LANES)
        table = pair_table(at[:, cut], ap[:, cut], asn[:, cut], own_a, rows, a_blocks)
        acodes[t * HALF : (t + 1) * HALF, :] = fold(table, LANES)[:HALF]
    matrix[...] = jnp.zeros_like(matrix)
    rowid = lax.broadcasted_iota(jnp.int32, (rows, LANES), 0)

    def fetch(place):
        return (rowid == place).astype(F32)

    def step(i, carry):
        cs = acodes[pl.ds(pl.multiple_of(i * GROUP, GROUP), GROUP), :]
        summed = contribution(cs, excite, fetch, True, wide, 1, count)
        matrix[...] += summed[:rows] + summed[rows:]
        return carry

    lax.fori_loop(0, acodes.shape[0] // GROUP, step, 0)


def beta_kernel(excite, slots, integrals, codes, *refs):
    ins, outs = refs[:slots], refs[slots : 2 * slots]
    wide, lookup, acc = refs[2 * slots :]
    rows, block = ins[0].shape
    fill_integrals(integrals, wide)
    for m in range(slots):
        lookup[:, m * block : (m + 1) * block] = ins[m][...]
    acc[...] = jnp.zeros_like(acc)
    total = slots * block
    chunks = acc.shape[0] // (2 * rows)

    def fetch(place):
        index = jnp.broadcast_to(place & (LANES - 1), (rows, LANES))
        tile = place // LANES
        value = jnp.zeros((rows, LANES), F32)
        for k in range(total // LANES):
            found = jnp.take_along_axis(
                lookup[:, k * LANES : (k + 1) * LANES], index, axis=1, mode="promise_in_bounds"
            )
            value = jnp.where(tile == k, found, value)
        return value

    def step(i, carry):
        cs = codes[pl.ds(pl.multiple_of(i * GROUP, GROUP), GROUP), :]
        acc[...] += contribution(cs, excite, fetch, False, wide, chunks, WIDE)
        return carry

    lax.fori_loop(0, codes.shape[0] // GROUP, step, 0)
    for c in range(chunks):
        base = 2 * rows * c
        lookup[:, c * WIDE : (c + 1) * WIDE] = acc[base : base + rows, :] + acc[base + rows : base + 2 * rows, :]
    for m in range(slots):
        outs[m][...] = lookup[:, m * block : (m + 1) * block]


def alpha_kernel(matrix, gathered, out):
    left_high, left_low = parts(matrix[...])
    high, low = parts(gathered[...])
    out[...] = nn(left_high, high) + nn(left_high, low) + nn(left_low, high)


def final_kernel(*refs):
    total = refs[0][...]
    for ref in refs[1:-1]:
        total = total + ref[...]
    refs[-1][...] = total


def swap(value, axis, size, mask):
    return lax.ppermute(value, axis, [(i, i ^ mask) for i in range(size)])


def local(a_blocks, b_blocks, vector, integrals, at, ap, asn, bt, bp, bsn):
    rows, block = vector.shape
    excite, count = at.shape
    received = [swap(vector, "beta", b_blocks, m) for m in range(b_blocks - 1, 0, -1)][::-1]
    half = block // 2
    vm = pl.BlockSpec(memory_space=pltpu.VMEM)
    codes, matrix = pl.pallas_call(
        functools.partial(prepare, excite, rows, block, a_blocks, b_blocks),
        out_shape=(
            jax.ShapeDtypeStruct((half, LANES), jnp.int32),
            jax.ShapeDtypeStruct((rows, count), F32),
        ),
        in_specs=[vm] * 7,
        out_specs=(vm, vm),
        scratch_shapes=[
            pltpu.VMEM((WIDE, 2 * WIDE), BF16),
            pltpu.VMEM((count // 2, LANES), jnp.int32),
        ],
        name="prepare",
    )(integrals, at, ap, asn, bt, bp, bsn)
    gathered = vector
    mask = 1
    while mask < a_blocks:
        gathered = jnp.concatenate([gathered, swap(gathered, "alpha", a_blocks, mask)], axis=0)
        mask *= 2
    total = b_blocks * block
    chunks = total // WIDE
    outs = pl.pallas_call(
        functools.partial(beta_kernel, excite, b_blocks),
        out_shape=[jax.ShapeDtypeStruct((rows, block), F32)] * b_blocks,
        in_specs=[vm] * (2 + b_blocks),
        out_specs=[vm] * b_blocks,
        scratch_shapes=[
            pltpu.VMEM((2 * WIDE, WIDE), BF16),
            pltpu.VMEM((rows, total), F32),
            pltpu.VMEM((2 * rows * chunks, WIDE), F32),
        ],
        name="beta",
    )(integrals, codes, vector, *received)
    back = [swap(outs[m], "beta", b_blocks, m) for m in range(b_blocks - 1, 0, -1)]
    alpha_part = pl.pallas_call(
        alpha_kernel,
        out_shape=jax.ShapeDtypeStruct((rows, block), F32),
        in_specs=[vm] * 2,
        out_specs=vm,
        name="alpha",
    )(matrix, gathered)
    return pl.pallas_call(
        final_kernel,
        out_shape=jax.ShapeDtypeStruct((rows, block), F32),
        in_specs=[vm] * (len(back) + 2),
        out_specs=vm,
        name="final",
    )(outs[0], alpha_part, *back)


def solution(mesh):
    placed = (P("alpha", "beta"), P(), P(), P(), P(), P(), P(), P())
    return jax.shard_map(
        functools.partial(local, mesh.shape["alpha"], mesh.shape["beta"]),
        mesh=mesh,
        in_specs=placed,
        out_specs=P("alpha", "beta"),
        check_vma=False,
    )
```

```python
import functools

import jax
import jax.numpy as jnp
from jax import lax
from jax.experimental import pallas as pl
from jax.experimental.pallas import tpu as pltpu
from jax.sharding import PartitionSpec as P

LANES = 128
HALF = 64
WIDE = 256
GROUP = 16
CHUNK = 128
F32 = jnp.float32
BF16 = jnp.bfloat16

PARAMS = pltpu.CompilerParams(vmem_limit_bytes=16 * 1024 * 1024)


def nt(left, right):
    return lax.dot_general(left, right, (((1,), (1,)), ((), ())), preferred_element_type=F32)


def nn(left, right):
    return lax.dot_general(left, right, (((1,), (0,)), ((), ())), preferred_element_type=F32)


def parts(value):
    high = value.astype(BF16)
    low = (value - high.astype(F32)).astype(BF16)
    return high, low


def up(size, step):
    return -(-size // step) * step


def local_place(targets, own, block, blocks):
    owner = jnp.zeros_like(targets)
    for step in range(1, blocks):
        owner += (targets >= step * block).astype(jnp.int32)
    return ((owner ^ own) - owner) * block + targets


def pair_table(targets, pairs, signs, own, block, blocks):
    place = local_place(targets, own, block, blocks)
    code = place * 512 + pairs * 2 + (signs < 0).astype(jnp.int32)
    excite, width = code.shape
    filler = jnp.full((HALF - excite, width), 510, jnp.int32)
    return jnp.concatenate([code, filler], axis=0)


def fold(code, strings):
    half = strings // 2
    first = code[:, :LANES]
    second = pltpu.roll(code, (code.shape[1] - half) % code.shape[1], 1)[:, :LANES]
    return jnp.concatenate([first, second], axis=0).T


def fill_integrals(integrals_ref, wide_ref, turned):
    count = integrals_ref.shape[0]
    padded = jnp.pad(integrals_ref[...], ((0, WIDE - count), (0, WIDE - count)))
    high, low = parts(padded.T if turned else padded)
    wide_ref[:WIDE, :] = high
    wide_ref[WIDE : 2 * WIDE, :] = low
    if wide_ref.shape[0] > 2 * WIDE:
        wide_ref[2 * WIDE :, :] = high


def decode(codes, g, excite):
    code = codes[g : g + 1, :]
    lane = lax.broadcasted_iota(jnp.int32, (1, LANES), 1)
    real = (lane & (HALF - 1)) < excite
    sign = jnp.where(real, 1 - 2 * (code & 1), 0).astype(F32)
    return code >> 9, (code >> 1) & 255, sign


def put_density(codes, excite, pair_rows, fetch, exact, down_ref, density_ref):
    lane = lax.broadcasted_iota(jnp.int32, (1, LANES), 1)
    halves = [(lane < HALF).astype(F32).astype(BF16), (lane >= HALF).astype(F32).astype(BF16)]
    for g in range(0, GROUP, 2):
        hots, highs, lows = [], [], []
        for k in range(2):
            place, pair, sign = decode(codes, g + k, excite)
            hots.append((down_ref[:pair_rows, :] == pair).astype(F32).astype(BF16))
            value = fetch(place) * sign
            rows = value.shape[0]
            high, low = (value.astype(BF16), None) if exact else parts(value)
            empty = jnp.zeros_like(high)
            for half in halves:
                for held, out in ((high, highs), (low, lows)):
                    if held is not None:
                        out.append(jnp.concatenate([held * half, empty] if k == 0 else [empty, held * half], axis=1))
        one_hot = jnp.concatenate(hots, axis=1)
        dens = nt(jnp.concatenate(highs + lows, axis=0), one_hot)
        span = slice(2 * rows * g, 2 * rows * (g + 2))
        if exact:
            dens = dens.astype(BF16)
            density_ref[span, :pair_rows] = dens
            density_ref[span, WIDE : WIDE + pair_rows] = dens
        else:
            high, low = parts(dens[: 4 * rows] + dens[4 * rows :])
            density_ref[span, :pair_rows] = high
            density_ref[span, WIDE : WIDE + pair_rows] = high
            density_ref[span, 2 * WIDE : 2 * WIDE + pair_rows] = low


def scatter(codes, excite, rows, down_ref, image_ref, chunks, chunk_width):
    lane = lax.broadcasted_iota(jnp.int32, (1, LANES), 1)
    lefts, rights = [], []
    for g in range(GROUP):
        place, pair, sign = decode(codes, g, excite)
        base = 2 * rows * g
        index = jnp.broadcast_to(pair & (LANES - 1), (rows, LANES))
        upper = pair >= LANES
        picks = []
        for s in range(2):
            span = slice(base + s * rows, base + (s + 1) * rows)
            low_pick = jnp.take_along_axis(image_ref[span, :LANES], index, axis=1, mode="promise_in_bounds")
            high_pick = jnp.take_along_axis(image_ref[span, LANES:], index, axis=1, mode="promise_in_bounds")
            picks.append(jnp.where(upper, high_pick, low_pick))
        value = jnp.where(lane < HALF, picks[0], picks[1]) * sign
        high, low = parts(value)
        if chunks == 1:
            lefts.append(jnp.concatenate([high, low], axis=0))
            within = place
        else:
            within = place & (chunk_width - 1)
            pieces = []
            for c in range(chunks):
                inside = (place >= c * chunk_width) & (place < (c + 1) * chunk_width)
                mask = inside.astype(F32).astype(BF16)
                pieces += [high * mask, low * mask]
            lefts.append(jnp.concatenate(pieces, axis=0))
        rights.append((down_ref[:chunk_width, :] == within).astype(F32).astype(BF16))
    return nt(jnp.concatenate(lefts, axis=1), jnp.concatenate(rights, axis=1))


def run(codes_ref, excite, rows, fetch, exact, wide_ref, down_ref, density_ref, image_ref, acc_ref, pair_rows, chunk_width):
    steps = codes_ref.shape[0] // GROUP
    chunks = acc_ref.shape[0] // (2 * rows)
    padding = pair_rows // LANES * LANES
    for start in range(0, density_ref.shape[2], WIDE):
        density_ref[:, :, start + padding : start + WIDE] = jnp.zeros_like(
            density_ref[:, :, start + padding : start + WIDE]
        )
    down_ref[...] = lax.broadcasted_iota(jnp.int32, down_ref.shape, 0)
    for i in range(steps + 2):
        if i >= 2:
            part = scatter(codes_ref[(i - 2) * GROUP : (i - 1) * GROUP, :], excite, rows, down_ref, image_ref.at[i % 2], chunks, chunk_width)
            acc_ref[...] = part if i == 2 else acc_ref[...] + part
        if 1 <= i <= steps:
            image_ref[(i - 1) % 2] = nn(density_ref[(i - 1) % 2], wide_ref[...])
        if i < steps:
            put_density(codes_ref[i * GROUP : (i + 1) * GROUP, :], excite, pair_rows, fetch, exact, down_ref, density_ref.at[i % 2])


def prepare(excite, a_blocks, b_blocks, mine, partner, *refs):
    hbm, (codes, matrix, joined, turned), refs = refs[:7], refs[7:11], refs[11:]
    (integrals, at, ap, asn, bt, bp, bsn), sems, scratch = refs[:7], refs[7], refs[8:]
    wide, acodes, down, density, image, acc = scratch
    rows, block = mine.shape
    own_a = lax.axis_index("alpha")
    own_b = lax.axis_index("beta")
    window = bt.shape[1]
    start = jnp.minimum(own_b * block // LANES * LANES, hbm[4].shape[1] - window)
    start = pl.multiple_of(start, LANES)
    copies = [
        pltpu.make_async_copy(source if k < 4 else source.at[:, pl.ds(start, window)], target, sems.at[k])
        for k, (source, target) in enumerate(zip(hbm, refs[:7]))
    ]
    for copy in copies:
        copy.start()
    joined[:rows, :] = mine[...]
    joined[rows:, :] = partner[...]
    for copy in copies:
        copy.wait()
    fill_integrals(integrals, wide, False)
    fill_integrals(integrals, turned, True)
    table = pair_table(bt[...], bp[...], bsn[...], own_b, block, b_blocks)
    table = pltpu.roll(table, (window - (own_b * block - start)) % window, 1)
    codes[...] = fold(table, block)[: codes.shape[0]]
    count = at.shape[1]
    for t in range(count // LANES):
        cut = slice(t * LANES, (t + 1) * LANES)
        table = pair_table(at[:, cut], ap[:, cut], asn[:, cut], own_a, rows, a_blocks)
        acodes[t * HALF : (t + 1) * HALF, :] = fold(table, LANES)[:HALF]
    rowid = lax.broadcasted_iota(jnp.int32, (rows, LANES), 0)

    def fetch(place):
        return (rowid == place).astype(F32)

    pair_rows = up(integrals.shape[0], 16)
    run(acodes, excite, rows, fetch, True, wide, down, density, image, acc, pair_rows, count)
    matrix[...] = acc[:rows, :] + acc[rows:, :]


def beta_kernel(excite, slots, pair_rows, wide, codes, *refs):
    ins, outs = refs[:slots], refs[slots : 2 * slots]
    lookup, down, density, image, acc = refs[2 * slots :]
    rows, block = ins[0].shape
    for m in range(slots):
        lookup[:, m * block : (m + 1) * block] = ins[m][...]
    total = slots * block
    chunks = acc.shape[0] // (2 * rows)

    def fetch(place):
        index = jnp.broadcast_to(place & (LANES - 1), (rows, LANES))
        tile = place // LANES
        value = jnp.zeros((rows, LANES), F32)
        for k in range(total // LANES):
            found = jnp.take_along_axis(
                lookup[:, k * LANES : (k + 1) * LANES], index, axis=1, mode="promise_in_bounds"
            )
            value = jnp.where(tile == k, found, value)
        return value

    run(codes, excite, rows, fetch, False, wide, down, density, image, acc, pair_rows, total // chunks)
    width = total // chunks
    for c in range(chunks):
        base = 2 * rows * c
        lookup[:, c * width : (c + 1) * width] = acc[base : base + rows, :] + acc[base + rows : base + 2 * rows, :]
    for m in range(slots):
        outs[m][...] = lookup[:, m * block : (m + 1) * block]


def alpha_kernel(matrix, *refs):
    left_high, left_low = parts(matrix[...])
    high, low = parts(jnp.concatenate([ref[...] for ref in refs[:-1]], axis=0))
    refs[-1][...] = nn(left_high, high) + nn(left_high, low) + nn(left_low, high)


def swap(value, axis, size, mask):
    return lax.ppermute(value, axis, [(i, i ^ mask) for i in range(size)])


def local(a_blocks, b_blocks, vector, integrals, at, ap, asn, bt, bp, bsn):
    rows, block = vector.shape
    excite, count = at.shape
    orbital_pairs = integrals.shape[0]
    pair_rows = up(orbital_pairs, 16)
    half = block // 2
    total = b_blocks * block
    window = min(up(block + LANES - 1, LANES), total)
    chunks = total // CHUNK
    vm = pl.BlockSpec(memory_space=pltpu.VMEM)
    hbm = pl.BlockSpec(memory_space=pltpu.HBM)
    lists = [(excite, count)] * 3 + [(excite, window)] * 3
    received = [swap(vector, "beta", b_blocks, m) for m in range(b_blocks - 1, 0, -1)][::-1]
    partner = swap(vector, "alpha", a_blocks, 1)
    codes, matrix, joined, turned = pl.pallas_call(
        functools.partial(prepare, excite, a_blocks, b_blocks),
        out_shape=(
            jax.ShapeDtypeStruct((half, LANES), jnp.int32),
            jax.ShapeDtypeStruct((rows, count), F32),
            jax.ShapeDtypeStruct((2 * rows, block), F32),
            jax.ShapeDtypeStruct((3 * WIDE, WIDE), BF16),
        ),
        in_specs=[vm] * 2 + [hbm] * 7,
        out_specs=(vm,) * 4,
        scratch_shapes=[
            pltpu.VMEM(integrals.shape, F32),
            *[pltpu.VMEM(shape, jnp.int32) for shape in lists],
            pltpu.SemaphoreType.DMA((7,)),
            pltpu.VMEM((2 * WIDE, WIDE), BF16),
            pltpu.VMEM((count // 2, LANES), jnp.int32),
            pltpu.VMEM((max(WIDE, count), LANES), jnp.int32),
            pltpu.VMEM((2, 2 * rows * GROUP, 2 * WIDE), BF16),
            pltpu.VMEM((2, 2 * rows * GROUP, WIDE), F32),
            pltpu.VMEM((2 * rows, count), F32),
        ],
        compiler_params=PARAMS,
        cost_estimate=pl.CostEstimate(flops=4_000_000_000, bytes_accessed=1_000_000, transcendentals=0),
        name="prepare",
    )(vector, partner, *(pltpu.with_memory_space_constraint(x, pltpu.HBM) for x in (integrals, at, ap, asn, bt, bp, bsn)))
    spread = [swap(joined, "alpha", a_blocks, m) for m in range(2, a_blocks, 2)]
    outs = pl.pallas_call(
        functools.partial(beta_kernel, excite, b_blocks, pair_rows),
        out_shape=[jax.ShapeDtypeStruct((rows, block), F32)] * b_blocks,
        in_specs=[vm] * (2 + b_blocks),
        out_specs=[vm] * b_blocks,
        scratch_shapes=[
            pltpu.VMEM((rows, total), F32),
            pltpu.VMEM((WIDE, LANES), jnp.int32),
            pltpu.VMEM((2, 2 * rows * GROUP, 3 * WIDE), BF16),
            pltpu.VMEM((2, 2 * rows * GROUP, WIDE), F32),
            pltpu.VMEM((2 * rows * chunks, CHUNK), F32),
        ],
        compiler_params=PARAMS,
        cost_estimate=pl.CostEstimate(flops=8_000_000_000, bytes_accessed=1_000_000, transcendentals=0),
        name="beta",
    )(turned, codes, vector, *received)
    back = [swap(outs[m], "beta", b_blocks, m) for m in range(b_blocks - 1, 0, -1)]
    alpha_part = pl.pallas_call(
        alpha_kernel,
        out_shape=jax.ShapeDtypeStruct((rows, block), F32),
        in_specs=[vm] * (2 + len(spread)),
        out_specs=vm,
        compiler_params=PARAMS,
        cost_estimate=pl.CostEstimate(flops=50_000_000, bytes_accessed=100_000, transcendentals=0),
        name="alpha",
    )(matrix, joined, *spread)
    result = outs[0] + alpha_part
    for part in back:
        result = result + part
    return result


def solution(mesh):
    placed = (P("alpha", "beta"), P(), P(), P(), P(), P(), P(), P())
    return jax.shard_map(
        functools.partial(local, mesh.shape["alpha"], mesh.shape["beta"]),
        mesh=mesh,
        in_specs=placed,
        out_specs=P("alpha", "beta"),
        check_vma=False,
    )
```
